256 devices in a mesh: batch: 128 (over y, z, x_lo, core), span: 2 (over x_hi).
Axes of the slice: x: 4 (x_hi: 2, x_lo: 2; x = x_hi * 2 + x_lo), y: 4, z: 8, core: 2. Of those that a mesh axis runs over, the one named last changes fastest.
Arguments:
- image_tokens: bfloat16 [256, 256, 512], P('batch'), may hold values from -400 to 400
- captions: bfloat16 [2048, 512], P(('batch', 'span')), may hold values from -6 to 6
- owner: int32 [2048], P(('batch', 'span')), may hold values from 0 to 255
- w_query: bfloat16 [512, 512], replicated, may hold values from -0.25 to 0.25
- w_key: bfloat16 [512, 512], replicated, may hold values from -0.25 to 0.25
- w_value: bfloat16 [512, 512], replicated, may hold values from -0.25 to 0.25
- w_out: bfloat16 [512, 512], replicated, may hold values from -0.25 to 0.25
Outputs:
- caption_grad: float32 [2048, 512], P(('batch', 'span'))
- token_grad: float32 [256, 256, 512], P('batch')
The draws below stay inside these ranges and needn't reach their ends.
Inputs may be any that keep to these rules, and one draw needn't show every extreme that they name: `owner`: each caption names one image.
All inputs are finite; a program needn't handle non-finite values.
Results may differ from the reference program's by a relative error of at most 0.039.
The reference program's roundings to bfloat16 on the way count: a program that leaves them out, or rounds other values in their place, can miss the bound.
Values may be sent and summed in bfloat16 or wider, within the bound.
No kernel may reach another device: no remote copies, remote signals or barrier semaphores. Data moves between devices by JAX's collectives and lax.ppermute only.
A program may use at most 64 MiB of HBM per device.

```python
import math
import jax
import jax.numpy as jnp
from jax import lax

HEADS = 8
HEAD_DIM = 64
D = 512
PATCHES = 256
IMAGES = 256
CAPTIONS = 2048


def draw_image_tokens(key, part):
    base_key = jax.random.fold_in(key, 0)
    base = jax.random.truncated_normal(base_key, -6.0, 6.0, (IMAGES, PATCHES, D), jnp.float32)
    return base.astype(jnp.bfloat16)


def with_ends(drawn, rng, low, top_value):
    index_at = [jax.random.randint(jax.random.fold_in(rng, axis), (), 0, length) for axis, length in enumerate(drawn.shape)]
    main_axis = drawn.shape.index(max(drawn.shape))
    beside = index_at[:main_axis] + [(index_at[main_axis] + 1) % drawn.shape[main_axis]] + index_at[main_axis + 1:]
    return drawn.at[tuple(index_at)].set(low).at[tuple(beside)].set(top_value)


def block_levels(stream_key, dims, pieces, low, top_value):
    def one(dim, shards_of):
        heights = jax.random.uniform(jax.random.fold_in(jax.random.fold_in(stream_key, 6), dim), (shards_of,), jnp.float32, low / len(pieces), top_value / len(pieces))
        return jnp.repeat(jnp.exp(heights), dims[dim] // shards_of).reshape((-1,) + (1,) * (len(dims) - dim - 1))

    loudness = one(*pieces[0])
    for cut in pieces[1:]:
        loudness = loudness * one(*cut)
    return loudness


def normal_values(key, dims, spread, reach, cuts=(), kind=jnp.bfloat16):
    result = spread * jax.random.normal(key, dims, jnp.float32)
    if cuts:
        result = result * block_levels(key, dims, cuts, -0.22, 0.18)
    return jnp.clip(result, -reach, reach).astype(kind)


def setup_inputs(seed: int = 0) -> dict:
    streams_of = jax.random.split(jax.random.key(seed), 8)
    image_tokens = draw_image_tokens(jax.random.fold_in(streams_of[7], 71), 0)
    captions = normal_values(streams_of[1], (CAPTIONS, D), 1.0, 6.0, ((0, 256),))
    owner = with_ends(jax.random.randint(streams_of[2], (CAPTIONS,), 0, IMAGES), jax.random.fold_in(streams_of[2], 1), 0, IMAGES - 1).astype(jnp.int32)
    w_query = normal_values(streams_of[3], (D, D), D ** -0.5, 0.25)
    w_key = normal_values(streams_of[4], (D, D), D ** -0.5, 0.25)
    w_value = normal_values(streams_of[5], (D, D), D ** -0.5, 0.25)
    w_out = normal_values(streams_of[6], (D, D), D ** -0.5, 0.25)
    return {"image_tokens": image_tokens, "captions": captions, "owner": owner, "w_query": w_query, "w_key": w_key, "w_value": w_value, "w_out": w_out}


LOGIT_SCALE = 10.0
LOGIT_BIAS = -2.0
NORM_EPS = 1e-06

def pair_loss(query, keys, values, caption_f, w_out, owner_block, image_base):
    count = query.shape[0]
    images = keys.shape[0]
    patches = keys.shape[1]
    width = keys.shape[2]
    query_heads = query.reshape(count, HEADS, HEAD_DIM)
    key_heads = keys.reshape(images, patches, HEADS, HEAD_DIM)
    value_heads = values.reshape(images, patches, HEADS, HEAD_DIM)
    scores = jnp.einsum('che,iphe->cihp', query_heads, key_heads, preferred_element_type=jnp.float32) * HEAD_DIM ** (-0.5)
    weights = jax.nn.softmax(scores, axis=-1).astype(jnp.bfloat16)
    pooled = jnp.einsum('cihp,iphe->cihe', weights, value_heads, preferred_element_type=jnp.float32)
    pooled = pooled.reshape(count * images, width).astype(jnp.bfloat16)
    mixed = jnp.dot(pooled, w_out, preferred_element_type=jnp.float32).reshape(count, images, width)
    inner = lax.optimization_barrier(jnp.sum(mixed * caption_f[:, None, :], axis=-1))
    mixed_norm = jnp.sqrt(lax.optimization_barrier(jnp.sum(mixed * mixed, axis=-1)) + NORM_EPS)
    caption_norm = jnp.sqrt(lax.optimization_barrier(jnp.sum(caption_f * caption_f, axis=-1)) + NORM_EPS)
    cosine = inner / (mixed_norm * caption_norm[:, None])
    logits = LOGIT_SCALE * cosine + LOGIT_BIAS
    image_ids = image_base + jnp.arange(images, dtype=jnp.int32)
    labels = jnp.where(owner_block[:, None] == image_ids[None, :], 1.0, -1.0).astype(jnp.float32)
    return jnp.sum(jax.nn.softplus(-labels * logits))

def block_grads(caption_block, owner_block, keys, values, w_query, w_out, image_base):
    query = jnp.dot(caption_block, w_query, preferred_element_type=jnp.float32).astype(jnp.bfloat16)
    caption_f = caption_block.astype(jnp.float32)

    def local(query_in, keys_in, values_in, caption_in):
        return pair_loss(query_in, keys_in, values_in, caption_in, w_out, owner_block, image_base)
    value, pull = jax.vjp(local, query, keys, values, caption_f)
    grad_query, grad_keys, grad_values, grad_direct = pull(jnp.ones((), jnp.float32))
    return (value, grad_query, grad_keys.astype(jnp.float32), grad_values.astype(jnp.float32), grad_direct)

def reference(image_tokens, captions, owner, w_query, w_key, w_value, w_out):
    token_rows = image_tokens.reshape(IMAGES * PATCHES, D)
    keys = jnp.dot(token_rows, w_key, preferred_element_type=jnp.float32).astype(jnp.bfloat16).reshape(IMAGES, PATCHES, D)
    values = jnp.dot(token_rows, w_value, preferred_element_type=jnp.float32).astype(jnp.bfloat16).reshape(IMAGES, PATCHES, D)
    group = math.gcd(CAPTIONS, 16)

    def step(carry, item):
        grad_keys, grad_values = carry
        caption_block, owner_block = item
        value, grad_query, more_keys, more_values, grad_direct = block_grads(caption_block, owner_block, keys, values, w_query, w_out, 0)
        caption_part = grad_direct + jnp.dot(grad_query.astype(jnp.bfloat16), w_query.T, preferred_element_type=jnp.float32)
        return ((grad_keys + more_keys, grad_values + more_values), caption_part)
    init = (jnp.zeros((IMAGES, PATCHES, D), jnp.float32), jnp.zeros((IMAGES, PATCHES, D), jnp.float32))
    items = (captions.reshape(CAPTIONS // group, group, D), owner.reshape(CAPTIONS // group, group))
    (grad_keys, grad_values), caption_parts = lax.scan(step, init, items)
    caption_grad = 16.0 * caption_parts.reshape(CAPTIONS, D)
    keys_b = grad_keys.reshape(IMAGES * PATCHES, D).astype(jnp.bfloat16)
    values_b = grad_values.reshape(IMAGES * PATCHES, D).astype(jnp.bfloat16)
    token_part = jnp.dot(keys_b, w_key.T, preferred_element_type=jnp.float32)
    token_part = token_part + jnp.dot(values_b, w_value.T, preferred_element_type=jnp.float32)
    token_grad = (PATCHES * token_part).reshape(IMAGES, PATCHES, D)
    return (caption_grad, token_grad)
```

```python
import functools

import jax
import jax.numpy as jnp
from jax import lax
from jax.experimental import pallas as pl
from jax.experimental.pallas import tpu as pltpu
from jax.sharding import Mesh
from jax.sharding import PartitionSpec as P

HEADS = 8
D = 512
PATCHES = 256
WIDE = 640
F32 = jnp.float32
BF16 = jnp.bfloat16
BATCH = ("y", "z", "x_lo", "core")
BATCH_SPAN = ("y", "z", "x_lo", "core", "span")
FAR = ("y", "z", "x_lo")

LOGIT_SCALE = 10.0
LOGIT_BIAS = -2.0
NORM_EPS = 1e-06

NN = (((1,), (0,)), ((), ()))
NT = (((1,), (1,)), ((), ()))


def dot(a, b, dims):
    return lax.dot_general(a, b, dims, preferred_element_type=F32)


def pairs_kernel(
    base_ref, tokens_ref, captions_ref, w_query_ref, w_key_ref, w_value_ref, w_out_ref,
    caption_ref, token_ref,
    queries, grad_query, direct, keys, values, weights, grad_scores, inverse, grad_keys, grad_values,
):
    images = tokens_ref.shape[0]
    low = lax.broadcasted_iota(jnp.int32, (1, 128), 1) < 64
    half = (low, jnp.logical_not(low))
    zero = jnp.zeros((), BF16)
    captions = captions_ref[:, :D]
    queries[...] = dot(captions, w_query_ref[...], NN).astype(BF16) * jnp.asarray(0.125, BF16)
    grad_query[...] = jnp.zeros_like(grad_query)
    direct[...] = jnp.zeros_like(direct)

    def of_head(h):
        return slice(h * PATCHES, (h + 1) * PATCHES)

    def of_pair(p):
        return slice(2 * p * PATCHES, (2 * p + 2) * PATCHES)

    def lanes(p):
        return slice(p * 128, (p + 1) * 128)

    def image(i, _):
        tokens = tokens_ref[i]
        k = dot(tokens, w_key_ref[...], NN).astype(BF16)
        v = dot(tokens, w_value_ref[...], NN).astype(BF16)
        for h in range(HEADS):
            keys[of_head(h), :] = jnp.where(half[h % 2], k[:, lanes(h // 2)], zero)
            values[of_head(h), :] = jnp.where(half[h % 2], v[:, lanes(h // 2)], zero)
        q = queries[...]
        pooled = []
        for p in range(HEADS // 2):
            scale = []
            for h in (2 * p, 2 * p + 1):
                scores = dot(q[:, lanes(p)], keys[of_head(h), :], NT)
                e = jnp.exp(scores - jnp.max(scores, axis=1, keepdims=True))
                weights[:, of_head(h)] = e.astype(BF16)
                scale.append(1.0 / jnp.sum(e, axis=1, keepdims=True))
            inv = jnp.where(low, scale[0], scale[1])
            inverse[:, lanes(p)] = inv
            pooled.append(dot(weights[:, of_pair(p)], values[of_pair(p), :], NN) * inv)
        pooled = jnp.concatenate(pooled, axis=1)
        mixed = dot(pooled.astype(BF16), w_out_ref[...], NN)
        caption = captions_ref[:, :D].astype(F32)
        inner = jnp.sum(mixed * caption, axis=1, keepdims=True)
        mixed_inv = lax.rsqrt(jnp.sum(mixed * mixed, axis=1, keepdims=True) + NORM_EPS)
        caption_inv = lax.rsqrt(jnp.sum(caption * caption, axis=1, keepdims=True) + NORM_EPS)
        cosine = inner * mixed_inv * caption_inv
        owner = captions_ref[:, D:].astype(F32)[:, 0:1]
        label = jnp.where(owner == (base_ref[0] + i).astype(F32), 1.0, -1.0)
        logit = LOGIT_SCALE * cosine + LOGIT_BIAS
        g = -LOGIT_SCALE * label / (1.0 + jnp.exp(label * logit))
        across = g * mixed_inv * caption_inv
        grad_mixed = across * caption - (g * cosine * mixed_inv * mixed_inv) * mixed
        direct[...] += across * mixed - (g * cosine * caption_inv * caption_inv) * caption
        grad_pooled = dot(grad_mixed.astype(BF16), w_out_ref[...], NT) * inverse[...]
        product = grad_pooled * pooled
        grad_pooled = grad_pooled.astype(BF16)
        more = []
        for p in range(HEADS // 2):
            for h in (2 * p, 2 * p + 1):
                mean = jnp.sum(jnp.where(half[h % 2], product[:, lanes(p)], 0.0), axis=1, keepdims=True)
                grad_weights = dot(grad_pooled[:, lanes(p)], values[of_head(h), :], NT)
                grad_scores[:, of_head(h)] = (
                    weights[:, of_head(h)].astype(F32) * (grad_weights - mean)
                ).astype(BF16)
            more.append(dot(grad_scores[:, of_pair(p)], keys[of_pair(p), :], NN))
        grad_query[...] += jnp.concatenate(more, axis=1)
        grad_pooled_t = grad_pooled.T
        q_t = q.T
        for h in range(HEADS):
            rows = slice(h * 64, (h + 1) * 64)
            grad_values[rows, :] = dot(grad_pooled_t[rows, :], weights[:, of_head(h)], NN)
            grad_keys[rows, :] = dot(q_t[rows, :], grad_scores[:, of_head(h)], NN)
        token_ref[i] = (
            dot(grad_keys[...].astype(BF16).T, w_key_ref[...], NT)
            + dot(grad_values[...].astype(BF16).T, w_value_ref[...], NT)
        ).astype(token_ref.dtype)
        return 0

    lax.fori_loop(0, images, image, 0)
    caption_ref[...] = (
        direct[...] + dot((grad_query[...] * 0.125).astype(BF16), w_query_ref[...], NT)
    ).astype(caption_ref.dtype)


def pairs(base, tokens, captions, w_query, w_key, w_value, w_out):
    images, count = (tokens.shape[0], captions.shape[0])
    vmem = pl.BlockSpec(memory_space=pltpu.VMEM)
    return pl.pallas_call(
        pairs_kernel,
        out_shape=(
            jax.ShapeDtypeStruct((count, D), BF16),
            jax.ShapeDtypeStruct((images, PATCHES, D), BF16),
        ),
        in_specs=[pl.BlockSpec(memory_space=pltpu.SMEM)] + [vmem] * 6,
        out_specs=(vmem, vmem),
        scratch_shapes=[
            pltpu.VMEM((count, D), BF16),
            pltpu.VMEM((count, D), F32),
            pltpu.VMEM((count, D), F32),
            pltpu.VMEM((HEADS * PATCHES, 128), BF16),
            pltpu.VMEM((HEADS * PATCHES, 128), BF16),
            pltpu.VMEM((count, HEADS * PATCHES), BF16),
            pltpu.VMEM((count, HEADS * PATCHES), BF16),
            pltpu.VMEM((count, D), F32),
            pltpu.VMEM((D, PATCHES), F32),
            pltpu.VMEM((D, PATCHES), F32),
        ],
        compiler_params=pltpu.CompilerParams(vmem_limit_bytes=40 * 1024 * 1024),
        name="pairs",
    )(base, tokens, captions, w_query, w_key, w_value, w_out)


def swapped(x, axis):
    return lax.ppermute(x, axis, ((0, 1), (1, 0)))


def on_device(image_tokens, captions, owner, w_query, w_key, w_value, w_out):
    own_images = image_tokens.shape[0]
    rows = captions.shape[0]
    side = jnp.broadcast_to(owner.astype(BF16)[:, None], (rows, WIDE - D))
    packet = jnp.concatenate([captions, side], axis=1)
    peers = lax.axis_size(FAR)
    gathered = lax.all_to_all(
        jnp.broadcast_to(packet, (peers, rows, WIDE)), FAR, split_axis=0, concat_axis=0, tiled=True
    ).reshape(peers * rows, WIDE)
    core = lax.axis_index("core")
    other_tokens = swapped(image_tokens, "core")
    chip = lax.axis_index(FAR) * (2 * own_images)
    w = (w_query, w_key, w_value, w_out)
    other_base = (chip + (1 - core) * own_images).reshape(1)
    own_base = (chip + core * own_images).reshape(1)
    caption_other, token_other = pairs(other_base, other_tokens, gathered, *w)
    caption_own, token_own = pairs(own_base, image_tokens, gathered, *w)
    token = token_own.astype(F32) + swapped(token_other, "core").astype(F32)
    token = token + swapped(token.astype(BF16), "span").astype(F32)
    token_grad = PATCHES * token
    caption = (caption_other.astype(F32) + caption_own.astype(F32)).astype(BF16)
    arrived = lax.all_to_all(
        caption.reshape(peers, rows, D), FAR, split_axis=0, concat_axis=0, tiled=True
    )
    caption_grad = 16.0 * jnp.sum(arrived.astype(F32), axis=0)
    return (caption_grad, token_grad)


def solution(mesh):
    torus = Mesh(
        mesh.devices.reshape(4, 8, 2, 2, mesh.shape["span"]),
        BATCH_SPAN,
    )
    placed = (P(BATCH, None, None), P(BATCH_SPAN, None), P(BATCH_SPAN), P(), P(), P(), P())
    return jax.shard_map(
        on_device,
        mesh=torus,
        in_specs=placed,
        out_specs=(P(BATCH_SPAN, None), P(BATCH, None, None)),
        check_vma=False,
    )
```

```python
import functools

import jax
import jax.numpy as jnp
from jax import lax
from jax.experimental import pallas as pl
from jax.experimental.pallas import tpu as pltpu
from jax.sharding import Mesh
from jax.sharding import PartitionSpec as P

HEADS = 8
HEAD_DIM = 64
D = 512
PATCHES = 256
CHUNK = 256
WIDE = 640
F32 = jnp.float32
BF16 = jnp.bfloat16
BATCH = ("y", "z", "x_lo", "core")
BATCH_SPAN = ("y", "z", "x_lo", "core", "span")
FAR = ("y", "z", "x_lo")
PLANE = ("y", "z")

LOGIT_SCALE = 10.0
LOGIT_BIAS = -2.0
NORM_EPS = 1e-06
LOG2E = 1.4426950408889634

NN = (((1,), (0,)), ((), ()))
NT = (((1,), (1,)), ((), ()))


def dot(a, b, dims=NN):
    return lax.dot_general(a, b, dims, preferred_element_type=F32)


def head(h):
    return slice(h * HEAD_DIM, (h + 1) * HEAD_DIM)


def pair(h):
    return slice((h // 2) * 128, (h // 2 + 1) * 128)


def patches_of(h):
    return slice(h * PATCHES, (h + 1) * PATCHES)


def prepare_captions(packet_ref, w_query_ref, q_ref, qt_ref, cap_ref, side_ref):
    captions = packet_ref[:, :D]
    query = dot(captions, w_query_ref[...]).astype(BF16) * jnp.asarray(0.125, BF16)
    q_ref[...] = query
    qt_ref[...] = query.T
    cap_ref[...] = captions.T
    cap = cap_ref[...].astype(F32)
    norm = lax.rsqrt(jnp.sum(cap * cap, axis=0, keepdims=True) + NORM_EPS)
    owner = packet_ref[:, D:].T.astype(F32)
    side_ref[0:8, :] = owner[0:8, :]
    side_ref[8:16, :] = jnp.broadcast_to(norm, (8, CHUNK))


def fill_zeros(padded):
    zero = jnp.zeros((HEAD_DIM, CHUNK), BF16)
    for h in range(HEADS):
        high = 128 * h + 64 * (1 - h % 2)
        padded[high : high + 64, :] = zero


def prepare_image(kv, kz, va, kt, vt_ref):
    lane = lax.broadcasted_iota(jnp.int32, (1, 128), 1)
    low = lane < 64
    zero = jnp.zeros((), BF16)
    kt[...] = kv[:, :D].T
    vt = kv[:, D:].T
    one = jnp.ones((16, PATCHES), BF16)
    for h in range(HEADS):
        mine = low if h % 2 == 0 else jnp.logical_not(low)
        start = 64 * (1 - h % 2)
        fill = jnp.where((lane == start) | (lane == start + 1), 1.0, 0.0).astype(BF16)
        p = h // 2
        kz[patches_of(h), :] = jnp.where(mine, kv[:, 128 * p : 128 * p + 128], zero)
        va[patches_of(h), :] = jnp.where(mine, kv[:, D + 128 * p : D + 128 * p + 128], fill)
        vt_ref[80 * h : 80 * h + 64, :] = vt[head(h), :]
        vt_ref[80 * h + 64 : 80 * h + 80, :] = one


def unit(image_id, img, block, w_out_t, w_out, slot, dq, dd, dk, dv, fresh_cap, fresh_img):
    kz, va, kt, vt = img
    q, qt, cap, side = block
    es, ds, pooled_s, gz = slot
    invs = []

    def scores_of(h):
        return dot(q[:, pair(h)], kz[patches_of(h), :], NT)

    coming = scores_of(0)
    for h in range(HEADS):
        scores = coming
        if h + 1 < HEADS:
            coming = scores_of(h + 1)
        top = jnp.max(scores, axis=1, keepdims=True)
        e = jnp.exp2((scores - top) * LOG2E).astype(BF16)
        es[:, patches_of(h)] = e
        both = dot(vt[80 * h : 80 * h + 80, :], e, NT)
        inv = 1.0 / both[64:65, :]
        invs.append(inv)
        pooled_s[head(h), :] = both[0:64, :] * inv
        yield
    pooled = pooled_s[...]
    mixed = dot(w_out_t[...], pooled.astype(BF16))
    caption = cap[...].astype(F32)
    inner = jnp.sum(mixed * caption, axis=0, keepdims=True)
    mixed_inv = lax.rsqrt(jnp.sum(mixed * mixed, axis=0, keepdims=True) + NORM_EPS)
    caption_inv = side[8:9, :]
    cosine = inner * mixed_inv * caption_inv
    label = jnp.where(side[0:1, :] == image_id, 1.0, -1.0)
    logit = LOGIT_SCALE * cosine + LOGIT_BIAS
    g = -LOGIT_SCALE * label / (1.0 + jnp.exp(label * logit))
    across = g * mixed_inv * caption_inv
    grad_mixed = across * caption - (g * cosine * mixed_inv * mixed_inv) * mixed
    straight = across * mixed - (g * cosine * caption_inv * caption_inv) * caption
    if fresh_cap:
        dd[...] = straight
    else:
        dd[...] += straight
    grad_pooled = dot(w_out[...], grad_mixed.astype(BF16))
    row = lax.broadcasted_iota(jnp.int32, (16, 1), 0)
    gps = []
    for h in range(HEADS):
        gp = grad_pooled[head(h), :] * invs[h]
        mean = -jnp.sum(gp * pooled_s[head(h), :], axis=0, keepdims=True)
        gp = gp.astype(BF16)
        gps.append(gp)
        coarse = mean.astype(BF16).astype(F32)
        both = jnp.where(row == 0, coarse, jnp.where(row == 1, mean - coarse, 0.0)).astype(BF16)
        low = 128 * h + 64 * (h % 2)
        high = 128 * h + 64 * (1 - h % 2)
        gz[low : low + 64, :] = gp
        gz[high : high + 16, :] = both
    yield

    def weights_of(h):
        return dot(gz[128 * h : 128 * h + 128, :].T, va[patches_of(h), :], NT)

    coming = weights_of(0)
    for h in range(HEADS):
        gw = coming
        if h + 1 < HEADS:
            coming = weights_of(h + 1)
        e = es[:, patches_of(h)]
        gs = (e.astype(F32) * gw).astype(BF16)
        ds[:, patches_of(h)] = gs
        more = dot(kt[head(h), :], gs, NT)
        mv = dot(gps[h], e)
        mk = dot(qt[head(h), :], gs)
        if fresh_cap:
            dq[head(h), :] = more
        else:
            dq[head(h), :] += more
        if fresh_img:
            dk[head(h), :] = mk
            dv[head(h), :] = mv
        else:
            dk[head(h), :] += mk
            dv[head(h), :] += mv
        yield


def pipeline(units):
    step = HEADS + 1
    ahead = units[0]
    for _ in range(step):
        next(ahead)
    for n in range(len(units)):
        current = units[n]
        after = units[n + 1] if n + 1 < len(units) else None
        for _ in range(HEADS):
            next(current)
            if after is not None:
                next(after)
        if after is not None:
            next(after)


def slots(count=2):
    one = [
        pltpu.VMEM((CHUNK, HEADS * PATCHES), BF16),
        pltpu.VMEM((CHUNK, HEADS * PATCHES), BF16),
        pltpu.VMEM((D, CHUNK), F32),
        pltpu.VMEM((1024, CHUNK), BF16),
    ]
    return one * count


IMAGE_SCRATCH = [
    pltpu.VMEM((HEADS * PATCHES, 128), BF16),
    pltpu.VMEM((HEADS * PATCHES, 128), BF16),
    pltpu.VMEM((D, PATCHES), BF16),
    pltpu.VMEM((640, PATCHES), BF16),
]
VM = pl.BlockSpec(memory_space=pltpu.VMEM)
SM = pl.BlockSpec(memory_space=pltpu.SMEM)
PARAMS = pltpu.CompilerParams(vmem_limit_bytes=28 * 1024 * 1024)
BLOCK = (
    jax.ShapeDtypeStruct((CHUNK, D), BF16),
    jax.ShapeDtypeStruct((D, CHUNK), BF16),
    jax.ShapeDtypeStruct((D, CHUNK), BF16),
    jax.ShapeDtypeStruct((16, CHUNK), F32),
)
TOTAL = jax.ShapeDtypeStruct((D, CHUNK), F32)


def project_kernel(tokens, w_key, w_value, out):
    for i in range(2):
        out[i, :, :D] = dot(tokens[i], w_key[...]).astype(BF16)
        out[i, :, D:] = dot(tokens[i], w_value[...]).astype(BF16)


def project(tokens, w_key, w_value):
    return pl.pallas_call(
        project_kernel,
        out_shape=jax.ShapeDtypeStruct((2, PATCHES, 2 * D), BF16),
        in_specs=[VM] * 3,
        out_specs=VM,
        compiler_params=PARAMS,
        cost_estimate=pl.CostEstimate(flops=2 * 512 * 512 * 1024, bytes_accessed=2**21, transcendentals=0),
        name="project",
    )(tokens, w_key, w_value)


def images_of(kv, scratch):
    images = []
    for i in range(2):
        img = scratch[4 * i : 4 * i + 4]
        prepare_image(kv.at[i], *img)
        images.append(img)
    return images


def first_kernel(base, packet, kv, w_query, w_out_t, w_out, q, qt, cap, side, dq, dd, dkv, *s):
    block = (q, qt, cap, side)
    prepare_captions(packet, w_query, *block)
    images = images_of(kv, s[:8])
    s = s[8:]
    units = []
    for i in range(2):
        slot = s[4 * i : 4 * i + 4]
        fill_zeros(slot[3])
        units.append(
            unit(
                (base[0] + i).astype(F32), images[i], block, w_out_t, w_out, slot,
                dq, dd, dkv.at[i, 0], dkv.at[i, 1], i == 0, True,
            )
        )
    pipeline(units)


def first(base, packet, kv, w_query, w_out_t, w_out):
    return pl.pallas_call(
        first_kernel,
        out_shape=(*BLOCK, TOTAL, TOTAL, jax.ShapeDtypeStruct((2, 2, D, PATCHES), F32)),
        in_specs=[SM] + [VM] * 5,
        out_specs=(VM,) * 7,
        scratch_shapes=IMAGE_SCRATCH * 2 + slots(),
        compiler_params=PARAMS,
        cost_estimate=pl.CostEstimate(flops=2 * 10**9, bytes_accessed=2**22, transcendentals=2**20),
        name="first",
    )(base, packet, kv, w_query, w_out_t, w_out)


def second_kernel(
    base, packet, kv, w_query, w_out_t, w_out, qa, qta, capa, sidea, dqa_in, dda_in,
    q, qt, cap, side, dqa, dda, dqb, ddb, dkv_b, dk, dv, *s,
):
    block_a = (qa, qta, capa, sidea)
    block_b = (q, qt, cap, side)
    prepare_captions(packet, w_query, *block_b)
    images = images_of(kv, s[:8])
    s = s[8:]
    fill_zeros(s[3])
    fill_zeros(s[7])
    dqa[...] = dqa_in[...]
    dda[...] = dda_in[...]
    units = []
    for i in range(2):
        name = (base[0] + i).astype(F32)
        img = images[i]
        units.append(
            unit(name, img, block_a, w_out_t, w_out, s[0:4], dqa, dda, dk.at[i], dv.at[i], False, True)
        )
        units.append(
            unit(name, img, block_b, w_out_t, w_out, s[4:8], dqb, ddb, dk.at[i], dv.at[i], i == 0, False)
        )
    pipeline(units)
    for i in range(2):
        dkv_b[i, 0] = dk[i].astype(BF16)
        dkv_b[i, 1] = dv[i].astype(BF16)


def second(base, packet, kv, w_query, w_out_t, w_out, block_a, dqa, dda):
    return pl.pallas_call(
        second_kernel,
        out_shape=(*BLOCK, TOTAL, TOTAL, TOTAL, TOTAL, jax.ShapeDtypeStruct((2, 2, D, PATCHES), BF16)),
        in_specs=[SM] + [VM] * 11,
        out_specs=(VM,) * 9,
        scratch_shapes=[pltpu.VMEM((2, D, PATCHES), F32)] * 2 + IMAGE_SCRATCH * 2 + slots(),
        compiler_params=PARAMS,
        cost_estimate=pl.CostEstimate(flops=4 * 10**9, bytes_accessed=2**22, transcendentals=2**21),
        name="second",
    )(base, packet, kv, w_query, w_out_t, w_out, *block_a, dqa, dda)


def third_kernel(
    base, kv, w_query, w_key, w_value, w_out_t, w_out, q, qt, cap, side, dqa, dda, dqb_in, ddb_in, dkv_in, arrived,
    caption_out, token_out, dqb, ddb, dk, dv, *s,
):
    block = (q, qt, cap, side)
    images = images_of(kv, s[:8])
    s = s[8:]
    fill_zeros(s[3])
    fill_zeros(s[7])
    dqb[...] = dqb_in[...]
    ddb[...] = ddb_in[...]
    units = []
    for i in range(2):
        units.append(
            unit(
                (base[0] + i).astype(F32), images[i], block, w_out_t, w_out, s[4 * i : 4 * i + 4],
                dqb, ddb, dk.at[i], dv.at[i], False, True,
            )
        )
    pipeline(units)
    for i in range(2):
        gk = dkv_in[i, 0] + arrived[i, 0].astype(F32) + dk[i]
        gv = dkv_in[i, 1] + arrived[i, 1].astype(F32) + dv[i]
        token = dot(w_key[...], gk.astype(BF16)) + dot(w_value[...], gv.astype(BF16))
        token_out[i] = token.astype(BF16).T
    here = base[1]
    for where, dq, dd in ((here, dqa, dda), (1 - here, dqb, ddb)):
        total = dd[...] + dot(w_query[...], (dq[...] * 0.125).astype(BF16))
        caption_out[:, pl.ds(where, 1)] = total.astype(BF16).T.reshape(32, 1, 8, D)


def third(base, kv, w_query, w_key, w_value, w_out_t, w_out, block, dqa, dda, dqb, ddb, dkv, arrived):
    return pl.pallas_call(
        third_kernel,
        out_shape=(
            jax.ShapeDtypeStruct((32, 2, 8, D), BF16),
            jax.ShapeDtypeStruct((2, PATCHES, D), BF16),
        ),
        in_specs=[SM] + [VM] * 16,
        out_specs=(VM,) * 2,
        scratch_shapes=[pltpu.VMEM((D, CHUNK), F32)] * 2
        + [pltpu.VMEM((2, D, PATCHES), F32)] * 2
        + IMAGE_SCRATCH * 2
        + slots(),
        compiler_params=PARAMS,
        cost_estimate=pl.CostEstimate(flops=2 * 10**9, bytes_accessed=2**22, transcendentals=2**20),
        name="third",
    )(base, kv, w_query, w_key, w_value, w_out_t, w_out, *block, dqa, dda, dqb, ddb, dkv, arrived)


def swapped(x, axis):
    return lax.ppermute(x, axis, ((0, 1), (1, 0)))


def on_device(image_tokens, captions, owner, w_query, w_key, w_value, w_out):
    own_images = image_tokens.shape[0]
    rows = captions.shape[0]
    side = jnp.broadcast_to(owner.astype(BF16)[:, None], (rows, WIDE - D))
    packet = jnp.concatenate([captions, side], axis=1)
    peers = lax.axis_size(PLANE)
    near = lax.all_to_all(
        jnp.broadcast_to(packet, (peers, rows, WIDE)), PLANE, split_axis=0, concat_axis=0, tiled=True
    ).reshape(peers * rows, WIDE)
    kv_own = project(image_tokens, w_key, w_value)
    kv_other = swapped(kv_own, "core")
    far = swapped(near, "x_lo")
    w_out_t = w_out.T
    core = lax.axis_index("core")
    chip = lax.axis_index(FAR) * (2 * own_images)
    x_lo = lax.axis_index("x_lo")
    base_own = jnp.stack([chip + core * own_images, x_lo])
    base_other = jnp.stack([chip + (1 - core) * own_images, x_lo])
    *block_a, dqa, dda, dkv = first(base_own, near, kv_own, w_query, w_out_t, w_out)
    *block_b, dqa, dda, dqb, ddb, dkv_other = second(
        base_other, far, kv_other, w_query, w_out_t, w_out, block_a, dqa, dda
    )
    arrived = swapped(dkv_other, "core")
    caption, token = third(
        base_own, kv_own, w_query, w_key, w_value, w_out_t, w_out, block_b, dqa, dda, dqb, ddb, dkv, arrived
    )
    other_half = swapped(token, "span")
    token_grad = PATCHES * (token.astype(F32) + other_half.astype(F32))
    sent = lax.all_to_all(caption.reshape(2 * peers, rows, D), FAR, split_axis=0, concat_axis=0, tiled=True)
    caption_grad = 16.0 * jnp.sum(sent.astype(F32), axis=0)
    return (caption_grad, token_grad)


def solution(mesh):
    torus = Mesh(mesh.devices.reshape(4, 8, 2, 2, mesh.shape["span"]), BATCH_SPAN)
    placed = (P(BATCH, None, None), P(BATCH_SPAN, None), P(BATCH_SPAN), P(), P(), P(), P())
    return jax.shard_map(
        on_device,
        mesh=torus,
        in_specs=placed,
        out_specs=(P(BATCH_SPAN, None), P(BATCH, None, None)),
        check_vma=False,
    )
```
